512 devices in a mesh: mid: 64 (over y, z), fin: 8 (over x, core).
Axes of the slice: x: 4, y: 8, z: 8, core: 2. Of those that a mesh axis runs over, the one named last changes fastest.
Arguments:
- history: float32 [1024, 64, 64, 128], P('mid', 'fin'), may hold values from -6 to 6
- sigma: float32 [4, 1024, 64, 128], P(None, 'mid', 'fin'), may hold values from -0.01171875 to 0.01171875
- propagator: float32 [64, 128], replicated, may hold values from -0.375 to 0.375
Outputs:
- new_rows: float32 [4, 64, 64, 128], P(None, 'fin', 'mid')
The draws below stay inside these ranges and needn't reach their ends.
All inputs are finite; a program needn't handle non-finite values.
Results may differ from the reference program's by a relative error of at most 0.0003.
Values sent between devices are 32-bit elements; how exact they have to be, the bound alone decides.
No kernel may reach another device: no remote copies, remote signals or barrier semaphores. Data moves between devices by JAX's collectives and lax.ppermute only.
A program may use at most 128 MiB of HBM per device.

```python
import jax
import jax.numpy as jnp
from jax import lax

NO = 64
COLS_DEV = 8
STEPS = 4
H = 1024
NCOL = 64


def block_scale(stream_key, dims, split, least, high):
    gain, own = 1.0, jax.random.fold_in(stream_key, 6)
    for dim, blocks in split:
        steps = jnp.exp(jax.random.uniform(jax.random.fold_in(own, dim), (blocks,), jnp.float32, least / len(split), high / len(split)))
        gain = gain * jnp.repeat(steps, dims[dim] // blocks).reshape([-1 if axis == dim else 1 for axis in range(len(dims))])
    return gain


def noise(stream_key, extent, spread, most, pieces=(), kind=jnp.bfloat16):
    gain = block_scale(stream_key, extent, pieces, -0.22, 0.18) if pieces else 1.0
    entries = jax.random.normal(stream_key, extent, jnp.float32) * spread * gain
    return jnp.minimum(jnp.maximum(entries, -most), most).astype(kind)


def setup_inputs(seed: int = 0) -> dict:
    arg_keys = jax.random.split(jax.random.key(seed), 4)
    return {
        "history": noise(arg_keys[0], (H, NCOL, NO, 2 * NO), 1.0, 6.0, ((0, 64), (1, 8)), jnp.float32),
        "sigma": noise(arg_keys[1], (STEPS, H, NO, 2 * NO), (4 * NO * H) ** -0.5, 0.01171875, ((1, 64), (2, 8)), jnp.float32),
        "propagator": noise(arg_keys[2], (NO, 2 * NO), (4 * NO) ** -0.5, 0.375, (), jnp.float32),
    }


def turn_pair(block, axis):
    half = block.shape[-1] // 2
    turned = jnp.concatenate([-block[..., half:], block[..., :half]], axis=-1)
    return jnp.concatenate([block, turned], axis=axis)


def integral(kernel, block, keep):
    masked = block * keep[:, :, None, None]
    stacked = turn_pair(masked, 2)
    return jnp.einsum('sik,sckj->cij', kernel, stacked, precision=lax.Precision.HIGHEST)


def propagate(weight, latest):
    stacked = turn_pair(latest, 1)
    return jnp.einsum('ik,ckj->cij', weight, stacked, precision=lax.Precision.HIGHEST)


def reference(history, sigma, propagator):
    ncol = history.shape[1]
    width = history.shape[0]
    col_times = (jnp.arange(ncol, dtype=jnp.int32) * width) // ncol
    slots = jnp.arange(width, dtype=jnp.int32)
    state = history
    latest = history[width - 1]
    outputs = []
    groups = ncol // COLS_DEV
    for step in range(STEPS):
        slot_times = jnp.where(slots >= step, slots, slots + width)
        keep = (slot_times[:, None] >= col_times[None, :]).astype(jnp.float32)
        kernel = sigma[step]

        def block_terms(group):
            start = (group * COLS_DEV).astype(jnp.int32)
            block = lax.dynamic_slice_in_dim(state, start, COLS_DEV, 1)
            keep_block = lax.dynamic_slice_in_dim(keep, start, COLS_DEV, 1)
            return integral(kernel, block, keep_block)

        memory = lax.map(block_terms, jnp.arange(groups, dtype=jnp.int32))
        memory = memory.reshape(ncol, history.shape[2], history.shape[3])
        new_row = propagate(propagator, latest) + memory
        state = state.at[step].set(new_row)
        latest = new_row
        outputs.append(new_row)
    return jnp.stack(outputs)
```

```python
import jax
import jax.numpy as jnp
from jax import lax
from jax.experimental import pallas as pl
from jax.experimental.pallas import tpu as pltpu
from jax.sharding import Mesh, PartitionSpec as P

STEPS = 4
PAIRS = [(k, l) for k in range(1, STEPS) for l in range(k)]
HIGHEST = lax.Precision.HIGHEST


def split(value):
    high = value.astype(jnp.bfloat16)
    low = (value - high.astype(jnp.float32)).astype(jnp.bfloat16)
    return high, low


def turn(block):
    lanes = block.shape[-1]
    half = lanes // 2
    rolled = pltpu.roll(block, half, block.ndim - 1)
    lane = lax.broadcasted_iota(jnp.int32, block.shape, block.ndim - 1)
    return jnp.where(lane < half, -rolled, rolled)


def memory_kernel(mid_ref, kernels_ref, history_ref, memory_ref, high_ref, low_ref):
    step = pl.program_id(0)
    sources, steps, parts, rows, depth = kernels_ref.shape
    lanes = history_ref.shape[-1]

    @pl.when(step == 0)
    def _():
        high, low = split(kernels_ref[...].reshape(sources * steps * parts * rows, depth))
        high_ref[...] = high
        low_ref[...] = low

    block = jnp.concatenate(
        [history_ref[:, c].reshape(depth, lanes) for c in range(2)], axis=1
    )
    block_high, block_low = split(block)
    dot = lambda a, b: jnp.dot(a, b, preferred_element_type=jnp.float32)
    total = dot(high_ref[...], block_high) + (
        dot(low_ref[...], block_high) + dot(high_ref[...], block_low)
    )
    total = total.reshape(sources, steps, parts, rows, 2 * lanes)
    for c in range(2):
        column = total[..., c * lanes : (c + 1) * lanes]
        value = column[:, :, 0] + turn(column[:, :, 1])
        kept = mid_ref[0] >= mid_ref[1] + 2 * step + c
        value = jnp.where(kept, value, 0.0)
        for k in range(steps):
            memory_ref[k, :, c * lanes : (c + 1) * lanes] = value[:, k].reshape(
                sources * rows, lanes
            )


def memory_terms(where, kernels, history):
    sources, steps, parts, rows, depth = kernels.shape
    slots, cols, orbitals, lanes = history.shape
    height = sources * steps * parts * rows
    return pl.pallas_call(
        memory_kernel,
        grid_spec=pltpu.PrefetchScalarGridSpec(
            num_scalar_prefetch=1,
            grid=(cols // 2,),
            in_specs=[
                pl.BlockSpec(kernels.shape, lambda g, w: (0, 0, 0, 0, 0)),
                pl.BlockSpec((slots, 2, orbitals, lanes), lambda g, w: (0, g, 0, 0)),
            ],
            out_specs=pl.BlockSpec((steps, orbitals, 2 * lanes), lambda g, w: (0, 0, g)),
            scratch_shapes=[pltpu.VMEM((height, depth), jnp.bfloat16)] * 2,
        ),
        out_shape=jax.ShapeDtypeStruct((steps, orbitals, cols * lanes), jnp.float32),
        compiler_params=pltpu.CompilerParams(dimension_semantics=("arbitrary",)),
        cost_estimate=pl.CostEstimate(
            flops=6 * height * depth * cols * lanes,
            bytes_accessed=8 << 20,
            transcendentals=0,
        ),
        name="memory_terms",
    )(where, kernels, history)


def recursion_kernel(memory_ref, blocks_ref, propagator_ref, out_ref):
    steps, orbitals, width = memory_ref.shape
    lanes = propagator_ref.shape[-1]
    cols = width // lanes
    stacked = []
    for k in range(steps):
        value = memory_ref[k]
        if k:
            weights = []
            for l in range(k):
                weight = blocks_ref[:, PAIRS.index((k, l))].reshape(orbitals, lanes)
                if l == k - 1:
                    weight = weight + propagator_ref[...]
                weights.append(weight)
            value = value + jnp.dot(
                jnp.concatenate(weights, axis=1),
                jnp.concatenate(stacked, axis=0),
                preferred_element_type=jnp.float32,
                precision=HIGHEST,
            )
        columns = [value[:, c * lanes : (c + 1) * lanes] for c in range(cols)]
        if k < steps - 1:
            stacked.append(value)
            stacked.append(jnp.concatenate([turn(column) for column in columns], axis=1))
        for c in range(cols):
            out_ref[:, k, c, :] = columns[c]


def recursion(memory, blocks, propagator):
    steps, orbitals, width = memory.shape
    lanes = propagator.shape[-1]
    return pl.pallas_call(
        recursion_kernel,
        out_shape=jax.ShapeDtypeStruct((orbitals, steps, width // lanes, lanes), jnp.float32),
        cost_estimate=pl.CostEstimate(
            flops=12 * 6 * orbitals * 2 * orbitals * width,
            bytes_accessed=3 << 20,
            transcendentals=0,
        ),
        name="recursion",
    )(memory, blocks, propagator)


def from_everyone(shard, axis):
    length = lax.axis_size(axis)
    return lax.all_to_all(
        jnp.broadcast_to(shard[None], (length, *shard.shape)), axis, 0, 0, tiled=True
    )


def on_device(history, sigma, propagator):
    mid_count = lax.axis_size(("y", "z"))
    fin_count = lax.axis_size(("x", "core"))
    mid_index = lax.axis_index(("y", "z"))
    fin_index = lax.axis_index(("x", "core"))
    slots, cols, orbitals, lanes = history.shape
    rows = sigma.shape[2]
    assert (mid_count * slots) // (fin_count * cols) == slots

    blocks = jnp.stack([sigma[k, l] for k, l in PAIRS])
    blocks = from_everyone(blocks, "z")[0]
    blocks = from_everyone(blocks, "y")[0]
    blocks = from_everyone(blocks, ("x", "core"))

    slot_ids = mid_index * slots + jnp.arange(slots, dtype=jnp.int32)
    steps = jnp.arange(STEPS, dtype=jnp.int32)
    old = slot_ids[None, :] >= steps[:, None]
    newest = (slot_ids[None, :] == mid_count * slots - 1) & (steps[:, None] == 0)
    own_rows = lax.dynamic_slice_in_dim(propagator, fin_index * rows, rows, 0)
    kernels = jnp.where(old[:, :, None, None], sigma, 0.0)
    kernels = kernels + jnp.where(newest[:, :, None, None], own_rows, 0.0)
    kernels = kernels.reshape(STEPS, slots, rows, 2, orbitals)
    kernels = kernels.transpose(0, 3, 2, 1, 4).reshape(STEPS, 2, rows, slots * orbitals)
    kernels = from_everyone(kernels, ("x", "core"))

    where = jnp.stack([mid_index, fin_index * cols]).astype(jnp.int32)
    memory = memory_terms(where, kernels, history)
    terms = recursion(memory, blocks, propagator)
    arrived = lax.all_to_all(terms, ("y", "z"), 0, 0, tiled=True)
    return arrived.sum(axis=0)[:, :, None, :]


def solution(mesh):
    devices = mesh.devices.reshape(8, 8, 4, 2)
    mesh = Mesh(devices, ("y", "z", "x", "core"))
    mid, fin = ("y", "z"), ("x", "core")
    in_specs = (P(mid, fin, None, None), P(None, mid, fin, None), P())
    out_specs = P(None, fin, mid, None)
    return jax.shard_map(
        on_device, mesh=mesh, in_specs=in_specs, out_specs=out_specs, check_vma=False
    )
```

```python
import jax
import jax.numpy as jnp
from jax import lax
from jax.experimental import pallas as pl
from jax.experimental.pallas import tpu as pltpu
from jax.sharding import Mesh, PartitionSpec as P


STEPS = 4
AXES = ("y1", "y0", "z", "x", "core")
MID, FIN = AXES[:3], AXES[3:]
HIGHEST = lax.Precision.HIGHEST


def split(value):
    high = value.astype(jnp.bfloat16)
    low = (value - high.astype(jnp.float32)).astype(jnp.bfloat16)
    return high, low


def turn(block):
    lanes = block.shape[-1]
    half = lanes // 2
    rolled = pltpu.roll(block, half, block.ndim - 1)
    lane = lax.broadcasted_iota(jnp.int32, block.shape, block.ndim - 1)
    return jnp.where(lane < half, -rolled, rolled)


def memory_kernel(where_ref, sigma_ref, propagator_ref, history_ref, memory_ref, high_ref, low_ref):
    step = pl.program_id(0)
    sources, steps, slots, rows, lanes = sigma_ref.shape
    half = lanes // 2
    first_slot, mid_last, first_col, first_device, first_pair = (where_ref[n] for n in range(5))

    @pl.when(step == 0)
    def _():
        lane = lax.broadcasted_iota(jnp.int32, (rows, lanes), 1)
        for n in range(sources):
            own_rows = propagator_ref[n * rows : (n + 1) * rows, :]
            own_rows = jnp.where(mid_last == 1, own_rows, 0.0)
            for k in range(steps):
                for p in range(0, slots, 2):
                    pair = [sigma_ref[n, k, p], sigma_ref[n, k, p + 1]]
                    for q in range(2):
                        if p + q < k:
                            pair[q] = jnp.where(first_slot + p + q >= k, pair[q], 0.0)
                    if k == 0 and p + 2 == slots:
                        pair[1] = pair[1] + own_rows
                    real = jnp.where(lane < half, pair[0], pltpu.roll(pair[1], half, 1))
                    imag = jnp.where(lane < half, pltpu.roll(pair[0], half, 1), pair[1])
                    high, low = split(jnp.concatenate([real, imag], axis=0))
                    at = (
                        pl.ds((n * steps + k) * 2 * rows, 2 * rows),
                        pl.ds(p * half, lanes),
                    )
                    high_ref[at] = high
                    low_ref[at] = low

    depth = slots * half
    block = jnp.concatenate(
        [history_ref[:, c].reshape(depth, lanes) for c in range(2)], axis=1
    )
    block_high, block_low = split(block)
    dot = lambda a, b: jnp.dot(a, b, preferred_element_type=jnp.float32)
    total = dot(high_ref[...], block_high) + (
        dot(low_ref[...], block_high) + dot(high_ref[...], block_low)
    )
    total = total.reshape(sources, steps, 2, rows, 2 * lanes)
    for c in range(2):
        column = total[..., c * lanes : (c + 1) * lanes]
        value = column[:, :, 0] + turn(column[:, :, 1])
        kept = first_device >= first_col + 2 * (first_pair + step) + c
        value = jnp.where(kept, value, 0.0)
        for k in range(steps):
            memory_ref[c, k] = value[:, k].reshape(sources * rows, lanes)


def memory_terms(where, sigma, propagator, history, cols):
    sources, steps, _, rows, _ = sigma.shape
    slots, _, orbitals, lanes = history.shape
    height = sources * steps * 2 * rows
    depth = slots * orbitals
    whole = lambda array: pl.BlockSpec(array.shape, lambda g, w: (0,) * array.ndim)
    return pl.pallas_call(
        memory_kernel,
        grid_spec=pltpu.PrefetchScalarGridSpec(
            num_scalar_prefetch=1,
            grid=(cols // 2,),
            in_specs=[
                whole(sigma),
                whole(propagator),
                pl.BlockSpec((slots, 2, orbitals, lanes), lambda g, w: (0, w[4] + g, 0, 0)),
            ],
            out_specs=pl.BlockSpec((2, steps, orbitals, lanes), lambda g, w: (g, 0, 0, 0)),
            scratch_shapes=[pltpu.VMEM((height, depth), jnp.bfloat16)] * 2,
        ),
        out_shape=jax.ShapeDtypeStruct((cols, steps, orbitals, lanes), jnp.float32),
        compiler_params=pltpu.CompilerParams(dimension_semantics=("arbitrary",)),
        cost_estimate=pl.CostEstimate(
            flops=6 * height * depth * cols * lanes,
            bytes_accessed=6 << 20,
            transcendentals=0,
        ),
        name="memory_terms",
    )(where, sigma, propagator, history)


def recursion_kernel(own_ref, arrived_ref, blocks_ref, propagator_ref, out_ref):
    cols, steps, orbitals, lanes = own_ref.shape
    stacked = []
    for k in range(steps):
        columns = [own_ref[c, k] + arrived_ref[c, k] for c in range(cols)]
        if k:
            weights = []
            for l in range(k):
                weight = blocks_ref[:, k - 1, l].reshape(orbitals, lanes)
                if l == k - 1:
                    weight = weight + propagator_ref[...]
                weights.append(weight)
            update = jnp.dot(
                jnp.concatenate(weights, axis=1),
                jnp.concatenate(stacked, axis=0),
                preferred_element_type=jnp.float32,
                precision=HIGHEST,
            )
            columns = [
                columns[c] + update[:, c * lanes : (c + 1) * lanes] for c in range(cols)
            ]
        if k < steps - 1:
            stacked.append(jnp.concatenate(columns, axis=1))
            stacked.append(jnp.concatenate([turn(column) for column in columns], axis=1))
        for c in range(cols):
            out_ref[:, k * cols + c, :] = columns[c]


def recursion(own, arrived, blocks, propagator):
    cols, steps, orbitals, lanes = own.shape
    return pl.pallas_call(
        recursion_kernel,
        out_shape=jax.ShapeDtypeStruct((orbitals, steps * cols, lanes), jnp.float32),
        cost_estimate=pl.CostEstimate(
            flops=12 * 6 * orbitals * 2 * orbitals * cols * lanes,
            bytes_accessed=2 << 20,
            transcendentals=0,
        ),
        name="recursion",
    )(own, arrived, blocks, propagator)


def from_everyone(shard, axis):
    length = lax.axis_size(axis)
    return lax.all_to_all(
        jnp.broadcast_to(shard[None], (length, *shard.shape)), axis, 0, 0, tiled=True
    )


def from_first(shard, axis, index):
    total = jnp.where(index == 0, shard, 0.0)
    for n in range(1, lax.axis_size(axis)):
        total = total + lax.ppermute(shard, axis, [(0, n)])
    return total


def on_device(history, sigma, propagator):
    y1s, y0s, zs, chips, cores = (lax.axis_size(axis) for axis in AXES)
    y1, y0, z, x, core = (lax.axis_index(axis) for axis in AXES)
    mid_index = (y1 * y0s + y0) * zs + z
    mid_count = y1s * y0s * zs
    fin_index = x * cores + core
    slots, cols, _, lanes = history.shape
    assert mid_count == chips * cores * cols and y0s == 2 and cols % 4 == 0

    sigmas = from_everyone(sigma, FIN)

    blocks = from_first(sigma[1:, : STEPS - 1], "z", z)
    blocks = from_first(blocks, ("y1", "y0"), y1 * y0s + y0)

    last = (mid_index == mid_count - 1).astype(jnp.int32)
    common = [mid_index * slots, last, fin_index * cols, mid_index]
    place = lambda pair: jnp.stack([jnp.asarray(n, jnp.int32) for n in common + [pair]])

    half = cols // 2
    pairs = half // 2
    sent = memory_terms(place((1 - y0) * pairs), sigmas, propagator, history, half)
    arrived = lax.ppermute(sent, "y0", [(0, 1), (1, 0)])
    blocks = from_everyone(blocks, FIN)
    own = memory_terms(place(y0 * pairs), sigmas, propagator, history, half)

    terms = recursion(own, arrived, blocks, propagator)
    arrived = lax.all_to_all(terms, MID, 0, 0, tiled=True)
    rows = arrived.reshape(y1s, y0s, zs, STEPS, half, lanes).sum(axis=(0, 2))
    return rows.transpose(1, 0, 2, 3).reshape(STEPS, cols, 1, lanes)


def solution(mesh):
    devices = mesh.devices.reshape(4, 2, 8, 4, 2)
    mesh = Mesh(devices, AXES)
    in_specs = (P(MID, FIN, None, None), P(None, MID, FIN, None), P())
    out_specs = P(None, FIN, MID, None)

    return jax.shard_map(
        on_device, mesh=mesh, in_specs=in_specs, out_specs=out_specs, check_vma=False
    )
```

```python
import jax
import jax.numpy as jnp
from jax import lax
from jax.experimental import pallas as pl
from jax.experimental.pallas import tpu as pltpu
from jax.sharding import Mesh, PartitionSpec as P


STEPS = 4
AXES = ("y1", "y0", "z", "x", "core")
MID, FIN = AXES[:3], AXES[3:]
HIGHEST = lax.Precision.HIGHEST


def split(value):
    high = value.astype(jnp.bfloat16)
    low = (value - high.astype(jnp.float32)).astype(jnp.bfloat16)
    return high, low


def turn(block):
    lanes = block.shape[-1]
    half = lanes // 2
    rolled = pltpu.roll(block, half, block.ndim - 1)
    lane = lax.broadcasted_iota(jnp.int32, block.shape, block.ndim - 1)
    return jnp.where(lane < half, -rolled, rolled)


def format_kernel(where_ref, sigma_ref, own_rows_ref, kernels_ref):
    steps, slots, rows, lanes = sigma_ref.shape
    half = lanes // 2
    first_slot, mid_last = where_ref[0], where_ref[1]
    lane = lax.broadcasted_iota(jnp.int32, (rows, lanes), 1)
    for k in range(steps):
        for p in range(0, slots, 2):
            pair = [sigma_ref[k, p], sigma_ref[k, p + 1]]
            for q in range(2):
                if p + q < k:
                    pair[q] = jnp.where(first_slot + p + q >= k, pair[q], 0.0)
            if k == 0 and p + 2 == slots:
                pair[1] = pair[1] + jnp.where(mid_last == 1, own_rows_ref[...], 0.0)
            real = jnp.where(lane < half, pair[0], pltpu.roll(pair[1], half, 1))
            imag = jnp.where(lane < half, pltpu.roll(pair[0], half, 1), pair[1])
            kernels_ref[0, k, 0, :, p * half : p * half + lanes] = real
            kernels_ref[0, k, 1, :, p * half : p * half + lanes] = imag


def formatted(where, sigma, propagator, copies):
    steps, slots, rows, lanes = sigma.shape
    block = (1, steps, 2, rows, slots * lanes // 2)
    return pl.pallas_call(
        format_kernel,
        grid_spec=pltpu.PrefetchScalarGridSpec(
            num_scalar_prefetch=1,
            grid=(copies,),
            in_specs=[
                pl.BlockSpec(sigma.shape, lambda g, w: (0, 0, 0, 0)),
                pl.BlockSpec((rows, lanes), lambda g, w: (w[2], 0)),
            ],
            out_specs=pl.BlockSpec(block, lambda g, w: (g, 0, 0, 0, 0)),
        ),
        out_shape=jax.ShapeDtypeStruct((copies, *block[1:]), jnp.float32),
        compiler_params=pltpu.CompilerParams(dimension_semantics=("arbitrary",)),
        cost_estimate=pl.CostEstimate(flops=1 << 20, bytes_accessed=2 << 20, transcendentals=0),
        name="formatted",
    )(where, sigma, propagator)


def memory_kernel(where_ref, same_ref, other_ref, history_ref, memory_ref, high_ref, low_ref):
    step = pl.program_id(0)
    chips, steps, parts, rows, depth = same_ref.shape
    lanes = history_ref.shape[-1]
    first_device, first_col, first_pair, core = (where_ref[n] for n in range(4))
    height = chips * steps * parts * rows

    @pl.when(step == 0)
    def _():
        for n, ref in enumerate((same_ref, other_ref)):
            high, low = split(ref[...].reshape(height, depth))
            high_ref[n * height : (n + 1) * height, :] = high
            low_ref[n * height : (n + 1) * height, :] = low

    block = jnp.concatenate(
        [history_ref[:, c].reshape(depth, lanes) for c in range(2)], axis=1
    )
    block_high, block_low = split(block)
    dot = lambda a, b: jnp.dot(a, b, preferred_element_type=jnp.float32)
    total = dot(high_ref[...], block_high) + (
        dot(low_ref[...], block_high) + dot(high_ref[...], block_low)
    )
    total = total.reshape(2, chips, steps, parts, rows, 2 * lanes)
    for c in range(2):
        column = total[..., c * lanes : (c + 1) * lanes]
        value = column[:, :, :, 0] + turn(column[:, :, :, 1])
        kept = first_device >= first_col + 2 * (first_pair + step) + c
        value = jnp.where(kept, value, 0.0)
        for n in range(2):
            owner = core if n == 0 else 1 - core
            for chip in range(chips):
                row = pl.multiple_of((2 * chip + owner) * rows, rows)
                memory_ref[c, :, pl.ds(row, rows), :] = value[n, chip]


def memory_terms(where, same, other, history, cols):
    chips, steps, parts, rows, depth = same.shape
    slots, _, orbitals, lanes = history.shape
    height = 2 * chips * steps * parts * rows
    whole = lambda array: pl.BlockSpec(array.shape, lambda g, w: (0,) * array.ndim)
    return pl.pallas_call(
        memory_kernel,
        grid_spec=pltpu.PrefetchScalarGridSpec(
            num_scalar_prefetch=1,
            grid=(cols // 2,),
            in_specs=[
                whole(same),
                whole(other),
                pl.BlockSpec((slots, 2, orbitals, lanes), lambda g, w: (0, w[2] + g, 0, 0)),
            ],
            out_specs=pl.BlockSpec((2, steps, orbitals, lanes), lambda g, w: (g, 0, 0, 0)),
            scratch_shapes=[pltpu.VMEM((height, depth), jnp.bfloat16)] * 2,
        ),
        out_shape=jax.ShapeDtypeStruct((cols, steps, orbitals, lanes), jnp.float32),
        compiler_params=pltpu.CompilerParams(dimension_semantics=("arbitrary",)),
        cost_estimate=pl.CostEstimate(
            flops=6 * height * depth * cols * lanes,
            bytes_accessed=6 << 20,
            transcendentals=0,
        ),
        name="memory_terms",
    )(where, same, other, history)


def recursion_kernel(own_ref, arrived_ref, blocks_ref, propagator_ref, out_ref):
    cols, steps, orbitals, lanes = own_ref.shape
    stacked = []
    for k in range(steps):
        columns = [own_ref[c, k] + arrived_ref[c, k] for c in range(cols)]
        if k:
            weights = []
            for l in range(k):
                weight = blocks_ref[:, k - 1, l].reshape(orbitals, lanes)
                if l == k - 1:
                    weight = weight + propagator_ref[...]
                weights.append(weight)
            update = jnp.dot(
                jnp.concatenate(weights, axis=1),
                jnp.concatenate(stacked, axis=0),
                preferred_element_type=jnp.float32,
                precision=HIGHEST,
            )
            columns = [
                columns[c] + update[:, c * lanes : (c + 1) * lanes] for c in range(cols)
            ]
        if k < steps - 1:
            stacked.append(jnp.concatenate(columns, axis=1))
            stacked.append(jnp.concatenate([turn(column) for column in columns], axis=1))
        for c in range(cols):
            out_ref[:, k * cols + c, :] = columns[c]


def recursion(own, arrived, blocks, propagator):
    cols, steps, orbitals, lanes = own.shape
    return pl.pallas_call(
        recursion_kernel,
        out_shape=jax.ShapeDtypeStruct((orbitals, steps * cols, lanes), jnp.float32),
        cost_estimate=pl.CostEstimate(
            flops=12 * 6 * orbitals * 2 * orbitals * cols * lanes,
            bytes_accessed=2 << 20,
            transcendentals=0,
        ),
        name="recursion",
    )(own, arrived, blocks, propagator)


def from_everyone(shard, axis):
    length = lax.axis_size(axis)
    return lax.all_to_all(
        jnp.broadcast_to(shard[None], (length, *shard.shape)), axis, 0, 0, tiled=True
    )


def from_first(shard, axis, index):
    total = jnp.where(index == 0, shard, 0.0)
    for n in range(1, lax.axis_size(axis)):
        total = total + lax.ppermute(shard, axis, [(0, n)])
    return total


def on_device(history, sigma, propagator):
    y1s, y0s, zs, chips, cores = (lax.axis_size(axis) for axis in AXES)
    y1, y0, z, x, core = (lax.axis_index(axis) for axis in AXES)
    mid_index = (y1 * y0s + y0) * zs + z
    mid_count = y1s * y0s * zs
    fin_index = x * cores + core
    slots, cols, _, lanes = history.shape
    assert mid_count == chips * cores * cols and y0s == 2 and cols % 4 == 0

    table = lambda *entries: jnp.stack([jnp.asarray(n, jnp.int32) for n in entries])
    last = (mid_index == mid_count - 1).astype(jnp.int32)

    kernels = formatted(table(mid_index * slots, last, fin_index), sigma, propagator, chips)
    same = lax.all_to_all(kernels, "x", 0, 0, tiled=True)
    other = lax.ppermute(same, "core", [(0, 1), (1, 0)])

    blocks = from_first(sigma[1:, : STEPS - 1], "z", z)
    blocks = from_everyone(blocks, ("y1", "y0"))[0]

    half = cols // 2
    pairs = half // 2
    place = lambda pair: table(mid_index, fin_index * cols, pair, core)
    sent = memory_terms(place((1 - y0) * pairs), same, other, history, half)
    arrived = lax.ppermute(sent, "y0", [(0, 1), (1, 0)])
    blocks = from_everyone(blocks, FIN)
    own = memory_terms(place(y0 * pairs), same, other, history, half)

    terms = recursion(own, arrived, blocks, propagator)
    arrived = lax.all_to_all(terms, MID, 0, 0, tiled=True)
    rows = arrived.reshape(y1s, y0s, zs, STEPS, half, lanes).sum(axis=(0, 2))
    return rows.transpose(1, 0, 2, 3).reshape(STEPS, cols, 1, lanes)


def solution(mesh):
    devices = mesh.devices.reshape(4, 2, 8, 4, 2)
    mesh = Mesh(devices, AXES)
    in_specs = (P(MID, FIN, None, None), P(None, MID, FIN, None), P())
    out_specs = P(None, FIN, MID, None)

    return jax.shard_map(
        on_device, mesh=mesh, in_specs=in_specs, out_specs=out_specs, check_vma=False
    )
```

```python
import jax
import jax.numpy as jnp
from jax import lax
from jax.experimental import pallas as pl
from jax.experimental.pallas import tpu as pltpu
from jax.sharding import Mesh, PartitionSpec as P


STEPS = 4
AXES = ("y1", "y0", "z", "x", "core")
MID, FIN = AXES[:3], AXES[3:]


def split(value):
    high = value.astype(jnp.bfloat16)
    low = (value - high.astype(jnp.float32)).astype(jnp.bfloat16)
    return high, low


def turn(block):
    lanes = block.shape[-1]
    half = lanes // 2
    rolled = pltpu.roll(block, half, block.ndim - 1)
    lane = lax.broadcasted_iota(jnp.int32, block.shape, block.ndim - 1)
    return jnp.where(lane < half, -rolled, rolled)


def in_vmem(array):
    return pltpu.with_memory_space_constraint(array, pltpu.VMEM)


def dot(a, b):
    return jnp.dot(a, b, preferred_element_type=jnp.float32)


def memory_kernel(where_ref, *refs):
    sigma_refs, (propagator_ref, history_ref, sent_ref, own_ref, high_ref, low_ref) = refs[:2], refs[2:]
    step = pl.program_id(0)
    chips, steps, slots, rows, lanes = sigma_refs[0].shape
    half = lanes // 2
    first_slot, mid_last, first_device, first_col, core, y0 = (where_ref[n] for n in range(6))

    def source_row(n, chip):
        owner = core if n == 0 else 1 - core
        return pl.multiple_of((2 * chip + owner) * rows, rows)

    @pl.when(step == 0)
    def _():
        lane = lax.broadcasted_iota(jnp.int32, (rows, lanes), 1)
        for n, ref in enumerate(sigma_refs):
            for chip in range(chips):
                own_rows = propagator_ref[pl.ds(source_row(n, chip), rows), :]
                own_rows = jnp.where(mid_last == 1, own_rows, 0.0)
                for k in range(steps):
                    for p in range(0, slots, 2):
                        pair = [ref[chip, k, p], ref[chip, k, p + 1]]
                        for q in range(2):
                            if p + q < k:
                                pair[q] = jnp.where(first_slot + p + q >= k, pair[q], 0.0)
                        if k == 0 and p + 2 == slots:
                            pair[1] = pair[1] + own_rows
                        real = jnp.where(lane < half, pair[0], pltpu.roll(pair[1], half, 1))
                        imag = jnp.where(lane < half, pltpu.roll(pair[0], half, 1), pair[1])
                        high, low = split(jnp.concatenate([real, imag], axis=0))
                        at = (
                            pl.ds(((n * chips + chip) * steps + k) * 2 * rows, 2 * rows),
                            pl.ds(p * half, lanes),
                        )
                        high_ref[at] = high
                        low_ref[at] = low

    depth = slots * half
    block = jnp.concatenate(
        [history_ref[:, c].reshape(depth, lanes) for c in range(2)], axis=1
    )
    block_high, block_low = split(block)
    total = dot(high_ref[...], block_high) + (
        dot(low_ref[...], block_high) + dot(high_ref[...], block_low)
    )
    total = total.reshape(2, chips, steps, 2, rows, 2 * lanes)
    pairs = pl.num_programs(0)
    first_pair = lax.rem(step + pairs // 2 * (1 - y0), pairs)

    def store(memory_ref):
        for c in range(2):
            column = total[..., c * lanes : (c + 1) * lanes]
            value = column[:, :, :, 0] + turn(column[:, :, :, 1])
            kept = first_device >= first_col + 2 * first_pair + c
            value = jnp.where(kept, value, 0.0)
            for n in range(2):
                for chip in range(chips):
                    memory_ref[c, :, pl.ds(source_row(n, chip), rows), :] = value[n, chip]

    @pl.when(step < pairs // 2)
    def _():
        store(sent_ref)

    @pl.when(step >= pairs // 2)
    def _():
        store(own_ref)


def memory_terms(where, same, other, propagator, history):
    chips, steps, slots, rows, lanes = same.shape
    _, cols, orbitals, _ = history.shape
    height = 2 * chips * steps * 2 * rows
    depth = slots * orbitals
    pairs = cols // 2
    whole = lambda array: pl.BlockSpec(array.shape, lambda g, w: (0,) * array.ndim)
    pair = lambda g, w: lax.rem(g + pairs // 2 * (1 - w[5]), pairs)
    block = (2, steps, orbitals, lanes)
    shape = jax.ShapeDtypeStruct((cols // 2, steps, orbitals, lanes), jnp.float32)
    return pl.pallas_call(
        memory_kernel,
        grid_spec=pltpu.PrefetchScalarGridSpec(
            num_scalar_prefetch=1,
            grid=(pairs,),
            in_specs=[
                pl.BlockSpec(memory_space=pltpu.VMEM),
                pl.BlockSpec(memory_space=pltpu.VMEM),
                whole(propagator),
                pl.BlockSpec((slots, 2, orbitals, lanes), lambda g, w: (0, pair(g, w), 0, 0)),
            ],
            out_specs=[
                pl.BlockSpec(block, lambda g, w: (jnp.minimum(g, pairs // 2 - 1), 0, 0, 0)),
                pl.BlockSpec(block, lambda g, w: (jnp.maximum(g - pairs // 2, 0), 0, 0, 0)),
            ],
            scratch_shapes=[pltpu.VMEM((height, depth), jnp.bfloat16)] * 2,
        ),
        out_shape=[shape, shape],
        compiler_params=pltpu.CompilerParams(dimension_semantics=("arbitrary",)),
        cost_estimate=pl.CostEstimate(
            flops=6 * height * depth * cols * lanes,
            bytes_accessed=8 << 20,
            transcendentals=0,
        ),
        name="memory_terms",
    )(where, *(in_vmem(array) for array in (same, other)), propagator, history)


def recursion_kernel(own_ref, arrived_ref, blocks_ref, propagator_ref, out_ref):
    cols, steps, orbitals, lanes = own_ref.shape
    stacked_high, stacked_low = [], []
    for k in range(steps):
        columns = [own_ref[c, k] + arrived_ref[c, k] for c in range(cols)]
        if k:
            weights = []
            for l in range(k):
                weight = blocks_ref[:, k - 1, l].reshape(orbitals, lanes)
                if l == k - 1:
                    weight = weight + propagator_ref[...]
                weights.append(weight)
            high, low = split(jnp.concatenate(weights, axis=1))
            update = dot(high, jnp.concatenate(stacked_high, axis=0)) + (
                dot(low, jnp.concatenate(stacked_high, axis=0))
                + dot(high, jnp.concatenate(stacked_low, axis=0))
            )
            columns = [
                columns[c] + update[:, c * lanes : (c + 1) * lanes] for c in range(cols)
            ]
        if k < steps - 1:
            for part in (columns, [turn(column) for column in columns]):
                high, low = split(jnp.concatenate(part, axis=1))
                stacked_high.append(high)
                stacked_low.append(low)
        for c in range(cols):
            out_ref[:, k * cols + c, :] = columns[c]


def recursion(own, arrived, blocks, propagator):
    cols, steps, orbitals, lanes = own.shape
    return pl.pallas_call(
        recursion_kernel,
        out_shape=jax.ShapeDtypeStruct((orbitals, steps * cols, lanes), jnp.float32),
        in_specs=[pl.BlockSpec(memory_space=pltpu.VMEM)] * 4,
        cost_estimate=pl.CostEstimate(
            flops=12 * 6 * orbitals * 2 * orbitals * cols * lanes,
            bytes_accessed=2 << 20,
            transcendentals=0,
        ),
        name="recursion",
    )(own, in_vmem(arrived), in_vmem(blocks), propagator)


def from_everyone(shard, axis):
    length = lax.axis_size(axis)
    return lax.all_to_all(
        jnp.broadcast_to(shard[None], (length, *shard.shape)), axis, 0, 0, tiled=True
    )


def from_first(shard, axis, index):
    total = jnp.where(index == 0, shard, 0.0)
    for n in range(1, lax.axis_size(axis)):
        total = total + lax.ppermute(shard, axis, [(0, n)])
    return total


def on_device(history, sigma, propagator):
    y1s, y0s, zs, chips, cores = (lax.axis_size(axis) for axis in AXES)
    y1, y0, z, x, core = (lax.axis_index(axis) for axis in AXES)
    mid_index = (y1 * y0s + y0) * zs + z
    mid_count = y1s * y0s * zs
    fin_index = x * cores + core
    slots, cols, _, lanes = history.shape
    assert mid_count == chips * cores * cols and y0s == 2 and cols % 4 == 0

    same = from_everyone(sigma, "x")
    other = lax.ppermute(same, "core", [(0, 1), (1, 0)])

    blocks = from_first(sigma[1:, : STEPS - 1], "z", z)
    blocks = from_everyone(blocks, ("y1", "y0"))[0]

    last = (mid_index == mid_count - 1).astype(jnp.int32)
    where = [mid_index * slots, last, mid_index, fin_index * cols, core, y0]
    where = jnp.stack([jnp.asarray(n, jnp.int32) for n in where])
    sent, own = memory_terms(where, same, other, propagator, history)
    arrived = lax.ppermute(sent, "y0", [(0, 1), (1, 0)])
    blocks = from_everyone(blocks, FIN)

    terms = recursion(own, arrived, blocks, propagator)
    arrived = lax.all_to_all(terms, MID, 0, 0, tiled=True)
    rows = arrived.reshape(y1s, y0s, zs, STEPS, cols // 2, lanes).sum(axis=(0, 2))
    return rows.transpose(1, 0, 2, 3).reshape(STEPS, cols, 1, lanes)


def solution(mesh):
    devices = mesh.devices.reshape(4, 2, 8, 4, 2)
    mesh = Mesh(devices, AXES)
    in_specs = (P(MID, FIN, None, None), P(None, MID, FIN, None), P())
    out_specs = P(None, FIN, MID, None)

    return jax.shard_map(
        on_device, mesh=mesh, in_specs=in_specs, out_specs=out_specs, check_vma=False
    )
```

```python
import functools

import jax
import jax.numpy as jnp
from jax import lax
from jax.experimental import pallas as pl
from jax.experimental.pallas import tpu as pltpu
from jax.sharding import Mesh, PartitionSpec as P


STEPS = 4
AXES = ("y1", "y0", "z1", "z0", "x", "core")
MID, FIN = AXES[:4], AXES[4:]
Y, Z = AXES[:2], AXES[2:4]


def split(value):
    high = value.astype(jnp.bfloat16)
    low = (value - high.astype(jnp.float32)).astype(jnp.bfloat16)
    return high, low


def turn(block):
    lanes = block.shape[-1]
    half = lanes // 2
    rolled = pltpu.roll(block, half, block.ndim - 1)
    lane = lax.broadcasted_iota(jnp.int32, block.shape, block.ndim - 1)
    return jnp.where(lane < half, -rolled, rolled)


def in_vmem(array):
    return pltpu.with_memory_space_constraint(array, pltpu.VMEM)


def in_hbm(array):
    return pltpu.with_memory_space_constraint(array, pltpu.HBM)


def dot(a, b):
    return jnp.dot(a, b, preferred_element_type=jnp.float32)


def position():
    mid_index, fin_index = 0, 0
    for axis in MID:
        mid_index = mid_index * lax.axis_size(axis) + lax.axis_index(axis)
    for axis in FIN:
        fin_index = fin_index * lax.axis_size(axis) + lax.axis_index(axis)
    return mid_index, fin_index


IN_VMEM = pl.BlockSpec(memory_space=pltpu.VMEM)


def spread_kernel(sigma_ref, kernels_ref, blocks_ref):
    for n in range(kernels_ref.shape[0]):
        kernels_ref[n] = sigma_ref[...]
    blocks_ref[...] = sigma_ref[1:, : STEPS - 1]


def copies_kernel(where, copies, *refs):
    own_ref, arrived_refs, out_ref = refs[0], refs[1:-1], refs[-1]
    index = sum(lax.axis_index(axis) for axis in where)
    total = jnp.where(index == 0, own_ref[...], 0.0)
    for ref in arrived_refs:
        total = total + ref[...]
    for n in range(copies):
        out_ref[n] = total


def first_kernel(arrived_ref, out_ref):
    for n in range(out_ref.shape[0]):
        out_ref[n] = arrived_ref[0]


def format_kernels(sigma_refs, propagator_ref, kernels_ref):
    chips, steps, slots, rows, lanes = sigma_refs[0].shape
    half = lanes // 2
    mid_index, _ = position()
    core = lax.axis_index("core")
    mid_count = lax.axis_size(MID)
    first_slot = mid_index * slots
    lane = lax.broadcasted_iota(jnp.int32, (rows, lanes), 1)
    for n, ref in enumerate(sigma_refs):
        for chip in range(chips):
            own_rows = propagator_ref[pl.ds(source_row(n, chip, core, rows), rows), :]
            own_rows = jnp.where(mid_index == mid_count - 1, own_rows, 0.0)
            for k in range(steps):
                for p in range(0, slots, 2):
                    pair = [ref[chip, k, p], ref[chip, k, p + 1]]
                    for q in range(2):
                        if p + q < k:
                            pair[q] = jnp.where(first_slot + p + q >= k, pair[q], 0.0)
                    if k == 0 and p + 2 == slots:
                        pair[1] = pair[1] + own_rows
                    real = jnp.where(lane < half, pair[0], pltpu.roll(pair[1], half, 1))
                    imag = jnp.where(lane < half, pltpu.roll(pair[0], half, 1), pair[1])
                    high, low = split(jnp.concatenate([real, imag], axis=0))
                    at = (
                        pl.ds(((n * chips + chip) * steps + k) * 2 * rows, 2 * rows),
                        pl.ds(p * half, lanes),
                    )
                    kernels_ref[(0, *at)] = high
                    kernels_ref[(1, *at)] = low


def source_row(n, chip, core, rows):
    owner = core if n == 0 else 1 - core
    return pl.multiple_of((2 * chip + owner) * rows, rows)


def add_terms(kernels_ref, history_ref, memory_ref, chips, pair):
    step = pl.program_id(0)
    _, steps, orbitals, lanes = memory_ref.shape
    depth = kernels_ref.shape[2]
    rows = orbitals // (2 * chips)
    mid_index, fin_index = position()
    core = lax.axis_index("core")
    first_col = (fin_index * 2 * pl.num_programs(0) + pair) * 2
    block = jnp.concatenate(
        [history_ref[:, c].reshape(depth, lanes) for c in range(2)], axis=1
    )
    block_high, block_low = split(block)
    total = dot(kernels_ref[0], block_high) + (
        dot(kernels_ref[1], block_high) + dot(kernels_ref[0], block_low)
    )
    total = total.reshape(2, chips, steps, 2, rows, 2 * lanes)
    for c in range(2):
        column = total[..., c * lanes : (c + 1) * lanes]
        value = column[:, :, :, 0] + turn(column[:, :, :, 1])
        value = jnp.where(mid_index >= first_col + c, value, 0.0)
        for n in range(2):
            for chip in range(chips):
                at = pl.ds(source_row(n, chip, core, rows), rows)
                memory_ref[2 * step + c, :, at, :] = value[n, chip]


def sent_kernel(chips, where_ref, same_ref, other_ref, propagator_ref, history_ref, memory_ref, kernels_ref):
    @pl.when(pl.program_id(0) == 0)
    def _():
        format_kernels((same_ref, other_ref), propagator_ref, kernels_ref)

    pair = pl.program_id(0) + pl.num_programs(0) * where_ref[0]
    add_terms(kernels_ref, history_ref, memory_ref, chips, pair)


def own_kernel(chips, where_ref, kernels_ref, history_ref, memory_ref):
    pair = pl.program_id(0) + pl.num_programs(0) * where_ref[0]
    add_terms(kernels_ref, history_ref, memory_ref, chips, pair)


def memory_terms(kernel, part, operands, small, history, chips, results):
    slots, cols, orbitals, lanes = history.shape
    steps, pairs = STEPS, cols // 4
    history_spec = pl.BlockSpec(
        (slots, 2, orbitals, lanes), lambda g, w: (0, g + pairs * w[0], 0, 0)
    )
    whole = lambda array: pl.BlockSpec(array.shape, lambda g, w: (0,) * array.ndim)
    shapes = [pltpu.VMEM((cols // 2, steps, orbitals, lanes), jnp.float32)]
    height = 2 * orbitals * steps
    shapes += [pltpu.VMEM((2, height, slots * orbitals), jnp.bfloat16)] * (results - 1)
    return pl.pallas_call(
        functools.partial(kernel, chips),
        grid_spec=pltpu.PrefetchScalarGridSpec(
            num_scalar_prefetch=1,
            grid=(pairs,),
            in_specs=[IN_VMEM] * len(operands)
            + [whole(array) for array in small]
            + [history_spec],
            out_specs=[IN_VMEM] * results,
        ),
        out_shape=shapes,
        compiler_params=pltpu.CompilerParams(
            dimension_semantics=("arbitrary",), vmem_limit_bytes=32 << 20
        ),
        cost_estimate=pl.CostEstimate(
            flops=6 * height * slots * orbitals * cols // 2 * lanes,
            bytes_accessed=3 << 20,
            transcendentals=0,
        ),
    )(part.reshape(1), *map(in_vmem, operands), *map(in_hbm, small), in_hbm(history))


def small_kernel(kernel, operands, shapes):
    return pl.pallas_call(
        kernel,
        in_specs=[IN_VMEM] * len(operands),
        out_specs=[IN_VMEM] * len(shapes),
        out_shape=[pltpu.VMEM(shape, jnp.float32) for shape in shapes],
        compiler_params=pltpu.CompilerParams(vmem_limit_bytes=32 << 20),
        cost_estimate=pl.CostEstimate(flops=1 << 16, bytes_accessed=1 << 18, transcendentals=0),
    )(*operands)


def half_kernel(own_ref, arrived_ref, sent_ref):
    cols = sent_ref.shape[0]
    at = pl.ds((1 - lax.axis_index("z0")) * cols, cols)
    sent_ref[...] = own_ref[at] + arrived_ref[at]


def recursion_kernel(own_ref, arrived_ref, last_ref, blocks_ref, propagator_ref, out_ref):
    cols, steps, orbitals, lanes = last_ref.shape
    first = lax.axis_index("z0") * cols
    stacked_high, stacked_low = [], []
    for k in range(steps):
        columns = [
            own_ref[first + c, k] + arrived_ref[first + c, k] + last_ref[c, k]
            for c in range(cols)
        ]
        if k:
            weights = []
            for l in range(k):
                weight = blocks_ref[:, k - 1, l].reshape(orbitals, lanes)
                if l == k - 1:
                    weight = weight + propagator_ref[...]
                weights.append(weight)
            high, low = split(jnp.concatenate(weights, axis=1))
            update = dot(high, jnp.concatenate(stacked_high, axis=0)) + (
                dot(low, jnp.concatenate(stacked_high, axis=0))
                + dot(high, jnp.concatenate(stacked_low, axis=0))
            )
            columns = [
                columns[c] + update[:, c * lanes : (c + 1) * lanes] for c in range(cols)
            ]
        if k < steps - 1:
            for part in (columns, [turn(column) for column in columns]):
                high, low = split(jnp.concatenate(part, axis=1))
                stacked_high.append(high)
                stacked_low.append(low)
        for c in range(cols):
            out_ref[:, k * cols + c, :] = columns[c]


def recursion(own, arrived, last, blocks, propagator):
    cols, steps, orbitals, lanes = last.shape
    return pl.pallas_call(
        recursion_kernel,
        out_shape=pltpu.VMEM((orbitals, steps * cols, lanes), jnp.float32),
        in_specs=[IN_VMEM] * 5,
        out_specs=IN_VMEM,
        compiler_params=pltpu.CompilerParams(vmem_limit_bytes=32 << 20),
        cost_estimate=pl.CostEstimate(
            flops=12 * 6 * orbitals * 2 * orbitals * cols * lanes,
            bytes_accessed=2 << 20,
            transcendentals=0,
        ),
        name="recursion",
    )(in_vmem(own), in_vmem(arrived), in_vmem(last), in_vmem(blocks), propagator)


def exchanged(parts, axis):
    return lax.all_to_all(parts, axis, 0, 0, tiled=True)


def on_device(history, sigma, propagator):
    y1s, y0s, z1s, z0s, chips, cores = (lax.axis_size(axis) for axis in AXES)
    ys, mid_count = y1s * y0s, y1s * y0s * z1s * z0s
    _, cols, _, lanes = history.shape
    assert mid_count == chips * cores * cols and y0s == z0s == 2 and cols % 8 == 0

    first = (STEPS - 1, STEPS - 1, *sigma.shape[2:])
    same, blocks = small_kernel(spread_kernel, [sigma], [(chips, *sigma.shape), first])
    same = exchanged(same, "x")
    other = lax.ppermute(same, "core", [(0, 1), (1, 0)])
    arrived = []
    for n in range(1, z1s * z0s):
        arrived.append(lax.ppermute(blocks, Z, [(0, n)]))
    kernel = functools.partial(copies_kernel, Z, ys)
    operands = [in_vmem(array) for array in (blocks, *arrived)]
    (blocks,) = small_kernel(kernel, operands, [(ys, *first)])
    blocks = exchanged(blocks, Y)

    y0 = lax.axis_index("y0")
    sent, kernels = memory_terms(
        sent_kernel, 1 - y0, [same], [other, propagator], history, chips, 2
    )
    arrived = lax.ppermute(sent, "y0", [(0, 1), (1, 0)])
    (blocks,) = small_kernel(first_kernel, [in_vmem(blocks)], [(chips * cores, *first)])
    blocks = exchanged(blocks, FIN)
    (own,) = memory_terms(own_kernel, y0, [kernels], [], history, chips, 1)

    operands = [in_vmem(own), in_vmem(arrived)]
    (sent,) = small_kernel(half_kernel, operands, [(cols // 4, *own.shape[1:])])
    last = lax.ppermute(sent, "z0", [(0, 1), (1, 0)])

    terms = recursion(own, arrived, last, blocks, propagator)
    arrived = exchanged(terms, MID)
    rows = arrived.reshape(y1s, y0s, z1s, z0s, STEPS, cols // 4, lanes).sum(axis=(0, 2))
    return rows.transpose(2, 0, 1, 3, 4).reshape(STEPS, cols, 1, lanes)


def solution(mesh):
    devices = mesh.devices.reshape(4, 2, 4, 2, 4, 2)
    mesh = Mesh(devices, AXES)
    in_specs = (P(MID, FIN, None, None), P(None, MID, FIN, None), P())
    out_specs = P(None, FIN, MID, None)

    return jax.shard_map(
        on_device, mesh=mesh, in_specs=in_specs, out_specs=out_specs, check_vma=False
    )
```

```python
import functools

import jax
import jax.numpy as jnp
from jax import lax
from jax.experimental import pallas as pl
from jax.experimental.pallas import tpu as pltpu
from jax.sharding import Mesh, PartitionSpec as P


STEPS = 4
AXES = ("y1", "y0", "z", "x", "core")
MID, FIN = AXES[:3], AXES[3:]


def split(value):
    high = value.astype(jnp.bfloat16)
    low = (value - high.astype(jnp.float32)).astype(jnp.bfloat16)
    return high, low


def turn(block):
    lanes = block.shape[-1]
    half = lanes // 2
    rolled = pltpu.roll(block, half, block.ndim - 1)
    lane = lax.broadcasted_iota(jnp.int32, block.shape, block.ndim - 1)
    return jnp.where(lane < half, -rolled, rolled)


def in_vmem(array):
    return pltpu.with_memory_space_constraint(array, pltpu.VMEM)


def in_hbm(array):
    return pltpu.with_memory_space_constraint(array, pltpu.HBM)


def dot(a, b):
    return jnp.dot(a, b, preferred_element_type=jnp.float32)


def position():
    y1, y0, z, x, core = (lax.axis_index(axis) for axis in AXES)
    y0s, zs, cores = (lax.axis_size(axis) for axis in ("y0", "z", "core"))
    return (y1 * y0s + y0) * zs + z, x * cores + core


IN_VMEM = pl.BlockSpec(memory_space=pltpu.VMEM)


def spread_kernel(sigma_ref, kernels_ref, blocks_ref):
    for n in range(kernels_ref.shape[0]):
        kernels_ref[n] = sigma_ref[...]
    blocks_ref[...] = sigma_ref[1:, : STEPS - 1]


def copies_kernel(where, copies, *refs):
    own_ref, arrived_refs, out_ref = refs[0], refs[1:-1], refs[-1]
    index = sum(lax.axis_index(axis) for axis in where)
    total = jnp.where(index == 0, own_ref[...], 0.0)
    for ref in arrived_refs:
        total = total + ref[...]
    for n in range(copies):
        out_ref[n] = total


def first_kernel(arrived_ref, out_ref):
    for n in range(out_ref.shape[0]):
        out_ref[n] = arrived_ref[0]


def format_kernels(sigma_refs, propagator_ref, kernels_ref):
    chips, steps, slots, rows, lanes = sigma_refs[0].shape
    half = lanes // 2
    mid_index, _ = position()
    core = lax.axis_index("core")
    mid_count = lax.axis_size(MID)
    first_slot = mid_index * slots
    lane = lax.broadcasted_iota(jnp.int32, (rows, lanes), 1)
    for n, ref in enumerate(sigma_refs):
        for chip in range(chips):
            own_rows = propagator_ref[pl.ds(source_row(n, chip, core, rows), rows), :]
            own_rows = jnp.where(mid_index == mid_count - 1, own_rows, 0.0)
            for k in range(steps):
                for p in range(0, slots, 2):
                    pair = [ref[chip, k, p], ref[chip, k, p + 1]]
                    for q in range(2):
                        if p + q < k:
                            pair[q] = jnp.where(first_slot + p + q >= k, pair[q], 0.0)
                    if k == 0 and p + 2 == slots:
                        pair[1] = pair[1] + own_rows
                    real = jnp.where(lane < half, pair[0], pltpu.roll(pair[1], half, 1))
                    imag = jnp.where(lane < half, pltpu.roll(pair[0], half, 1), pair[1])
                    high, low = split(jnp.concatenate([real, imag], axis=0))
                    at = (
                        pl.ds(((n * chips + chip) * steps + k) * 2 * rows, 2 * rows),
                        pl.ds(p * half, lanes),
                    )
                    kernels_ref[(0, *at)] = high
                    kernels_ref[(1, *at)] = low


def source_row(n, chip, core, rows):
    owner = core if n == 0 else 1 - core
    return pl.multiple_of((2 * chip + owner) * rows, rows)


def add_terms(kernels_ref, history_ref, memory_ref, chips, pair):
    step = pl.program_id(0)
    _, steps, orbitals, lanes = memory_ref.shape
    depth = kernels_ref.shape[2]
    rows = orbitals // (2 * chips)
    mid_index, fin_index = position()
    core = lax.axis_index("core")
    first_col = (fin_index * 2 * pl.num_programs(0) + pair) * 2
    block = jnp.concatenate(
        [history_ref[:, c].reshape(depth, lanes) for c in range(2)], axis=1
    )
    block_high, block_low = split(block)
    total = dot(kernels_ref[0], block_high) + (
        dot(kernels_ref[1], block_high) + dot(kernels_ref[0], block_low)
    )
    total = total.reshape(2, chips, steps, 2, rows, 2 * lanes)
    for c in range(2):
        column = total[..., c * lanes : (c + 1) * lanes]
        value = column[:, :, :, 0] + turn(column[:, :, :, 1])
        value = jnp.where(mid_index >= first_col + c, value, 0.0)
        for n in range(2):
            for chip in range(chips):
                at = pl.ds(source_row(n, chip, core, rows), rows)
                memory_ref[2 * step + c, :, at, :] = value[n, chip]


def sent_kernel(chips, where_ref, other_ref, same_ref, propagator_ref, history_ref, memory_ref, kernels_ref):
    @pl.when(pl.program_id(0) == 0)
    def _():
        format_kernels((same_ref, other_ref), propagator_ref, kernels_ref)

    pair = pl.program_id(0) + pl.num_programs(0) * where_ref[0]
    add_terms(kernels_ref, history_ref, memory_ref, chips, pair)


def own_kernel(chips, where_ref, kernels_ref, history_ref, memory_ref):
    pair = pl.program_id(0) + pl.num_programs(0) * where_ref[0]
    add_terms(kernels_ref, history_ref, memory_ref, chips, pair)


def memory_terms(kernel, part, operands, small, history, chips, results):
    slots, cols, orbitals, lanes = history.shape
    steps, pairs = STEPS, cols // 4
    history_spec = pl.BlockSpec(
        (slots, 2, orbitals, lanes), lambda g, w: (0, g + pairs * w[0], 0, 0)
    )
    whole = lambda array: pl.BlockSpec(array.shape, lambda g, w: (0,) * array.ndim)
    shapes = [pltpu.VMEM((cols // 2, steps, orbitals, lanes), jnp.float32)]
    height = 2 * orbitals * steps
    shapes += [pltpu.VMEM((2, height, slots * orbitals), jnp.bfloat16)] * (results - 1)
    return pl.pallas_call(
        functools.partial(kernel, chips),
        grid_spec=pltpu.PrefetchScalarGridSpec(
            num_scalar_prefetch=1,
            grid=(pairs,),
            in_specs=[IN_VMEM] * len(operands)
            + [whole(array) for array in small]
            + [history_spec],
            out_specs=[IN_VMEM] * results,
        ),
        out_shape=shapes,
        compiler_params=pltpu.CompilerParams(
            dimension_semantics=("arbitrary",), vmem_limit_bytes=32 << 20
        ),
        cost_estimate=pl.CostEstimate(
            flops=6 * height * slots * orbitals * cols // 2 * lanes,
            bytes_accessed=3 << 20,
            transcendentals=0,
        ),
    )(part.reshape(1), *map(in_vmem, operands), *map(in_hbm, small), in_hbm(history))


def small_kernel(kernel, operands, shapes):
    return pl.pallas_call(
        kernel,
        in_specs=[IN_VMEM] * len(operands),
        out_specs=[IN_VMEM] * len(shapes),
        out_shape=[pltpu.VMEM(shape, jnp.float32) for shape in shapes],
        compiler_params=pltpu.CompilerParams(vmem_limit_bytes=32 << 20),
        cost_estimate=pl.CostEstimate(flops=1 << 16, bytes_accessed=1 << 18, transcendentals=0),
    )(*operands)


def recursion_kernel(own_ref, arrived_ref, blocks_ref, propagator_ref, out_ref):
    cols, steps, orbitals, lanes = own_ref.shape
    stacked_high, stacked_low = [], []
    for k in range(steps):
        columns = [own_ref[c, k] + arrived_ref[c, k] for c in range(cols)]
        if k:
            weights = []
            for l in range(k):
                weight = blocks_ref[:, k - 1, l].reshape(orbitals, lanes)
                if l == k - 1:
                    weight = weight + propagator_ref[...]
                weights.append(weight)
            high, low = split(jnp.concatenate(weights, axis=1))
            update = dot(high, jnp.concatenate(stacked_high, axis=0)) + (
                dot(low, jnp.concatenate(stacked_high, axis=0))
                + dot(high, jnp.concatenate(stacked_low, axis=0))
            )
            columns = [
                columns[c] + update[:, c * lanes : (c + 1) * lanes] for c in range(cols)
            ]
        if k < steps - 1:
            for part in (columns, [turn(column) for column in columns]):
                high, low = split(jnp.concatenate(part, axis=1))
                stacked_high.append(high)
                stacked_low.append(low)
        for c in range(cols):
            out_ref[:, k * cols + c, :] = columns[c]


def recursion(own, arrived, blocks, propagator):
    cols, steps, orbitals, lanes = own.shape
    return pl.pallas_call(
        recursion_kernel,
        out_shape=pltpu.VMEM((orbitals, steps * cols, lanes), jnp.float32),
        in_specs=[IN_VMEM] * 4,
        out_specs=IN_VMEM,
        compiler_params=pltpu.CompilerParams(vmem_limit_bytes=32 << 20),
        cost_estimate=pl.CostEstimate(
            flops=12 * 6 * orbitals * 2 * orbitals * cols * lanes,
            bytes_accessed=2 << 20,
            transcendentals=0,
        ),
        name="recursion",
    )(in_vmem(own), in_vmem(arrived), in_vmem(blocks), propagator)


def exchanged(parts, axis):
    return lax.all_to_all(parts, axis, 0, 0, tiled=True)


def on_device(history, sigma, propagator):
    y1s, y0s, zs, chips, cores = (lax.axis_size(axis) for axis in AXES)
    mid_count = y1s * y0s * zs
    _, cols, _, lanes = history.shape
    assert mid_count == chips * cores * cols and y0s == 2 and cols % 4 == 0

    first = (STEPS - 1, STEPS - 1, *sigma.shape[2:])
    same, blocks = small_kernel(spread_kernel, [sigma], [(chips, *sigma.shape), first])
    same = exchanged(same, "x")
    other = lax.ppermute(same, "core", [(0, 1), (1, 0)])
    arrived = []
    for n in range(1, zs):
        arrived.append(lax.ppermute(blocks, "z", [(0, n)]))
    kernel = functools.partial(copies_kernel, ("z",), y1s * y0s)
    operands = [in_vmem(array) for array in (blocks, *arrived)]
    (blocks,) = small_kernel(kernel, operands, [(y1s * y0s, *first)])
    blocks = exchanged(blocks, ("y1", "y0"))

    y0 = lax.axis_index("y0")
    sent, kernels = memory_terms(
        sent_kernel, 1 - y0, [other], [same, propagator], history, chips, 2
    )
    arrived = lax.ppermute(sent, "y0", [(0, 1), (1, 0)])
    (blocks,) = small_kernel(first_kernel, [in_vmem(blocks)], [(chips * cores, *first)])
    blocks = exchanged(blocks, FIN)
    (own,) = memory_terms(own_kernel, y0, [kernels], [], history, chips, 1)

    terms = recursion(own, arrived, blocks, propagator)
    arrived = lax.all_to_all(terms, MID, 0, 0, tiled=True)
    rows = arrived.reshape(y1s, y0s, zs, STEPS, cols // 2, lanes).sum(axis=(0, 2))
    return rows.transpose(1, 0, 2, 3).reshape(STEPS, cols, 1, lanes)


def solution(mesh):
    devices = mesh.devices.reshape(4, 2, 8, 4, 2)
    mesh = Mesh(devices, AXES)
    in_specs = (P(MID, FIN, None, None), P(None, MID, FIN, None), P())
    out_specs = P(None, FIN, MID, None)

    return jax.shard_map(
        on_device, mesh=mesh, in_specs=in_specs, out_specs=out_specs, check_vma=False
    )
```
